32 devices in a mesh: item: 16 (over z, x, core), grp: 2 (over y).
Axes of the slice: x: 2, y: 2, z: 4, core: 2. Of those that a mesh axis runs over, the one named last changes fastest.
Arguments:
- hidden: bfloat16 [768, 256], P(('grp', 'item')), may hold values from -400 to 400
- item_table: bfloat16 [131072, 256], P('item'), may hold values from -1.5 to 1.5
- targets: int32 [768], P(('grp', 'item')), may hold values from 0 to 131071
- lengths: int32 [2, 16], replicated, may hold values from 1 to 96, 384 in all within a row
Outputs:
- row_loss: float32 [768], P(('grp', 'item'))
- hidden_grad: bfloat16 [768, 256], P(('grp', 'item'))
- table_grad: bfloat16 [131072, 256], P(('item', 'grp'))
The draws below stay inside these ranges and needn't reach their ends.
Inputs may be any that keep to these rules, and one draw needn't show every extreme that they name: Each row holds the lengths of the 16 user sequences that fill one group's 384 positions in order, and sums to 384.
All inputs are finite; a program needn't handle non-finite values.
Results may differ from the reference program's by a relative error of at most 0.0047.
Values may be sent and summed in bfloat16 or wider, within the bound.
A program may use at most 64 MiB of HBM per device.

```python
import math
import jax
import jax.numpy as jnp
import numpy as np
from jax import lax

D = 256
ITEM_DEV = 8192
TOKG = 384
SEQG = 16
TOKENS = 768
ITEMS = 131072
MAXLEN = 96
N_GRP = 2


def draw_common(key):
    table_key = jax.random.fold_in(jax.random.fold_in(key, 7), 0)
    state_key = jax.random.fold_in(jax.random.fold_in(key, 7), 1)
    item_key = jax.random.fold_in(jax.random.fold_in(key, 7), 3)
    noise_key = jax.random.fold_in(jax.random.fold_in(key, 7), 4)
    place_key = jax.random.fold_in(jax.random.fold_in(key, 7), 5)
    table = 0.2 * jax.random.truncated_normal(table_key, -5.0, 5.0, (ITEMS, D), jnp.float32)
    states = jax.random.truncated_normal(state_key, -6.0, 6.0, (TOKENS, D), jnp.float32)
    chosen = jax.random.randint(item_key, (8,), 0, ITEMS // 2)
    partner = chosen + ITEMS // 2
    strength = jnp.array([120.0, 220.0, 300.0, 160.0, 260.0, 120.0, 220.0, 300.0], jnp.float32)
    anchor = table[chosen]
    anchor_sq = jnp.sum(anchor * anchor, axis=1, keepdims=True)
    noise = jax.random.normal(noise_key, (8, D), jnp.float32)
    noise = noise - jnp.sum(noise * anchor, axis=1, keepdims=True) / anchor_sq * anchor
    partner_rows = anchor * (1.0 + 2.0 / strength[:, None]) + 0.05 * jnp.clip(noise, -5.0, 5.0)
    table = table.at[partner].set(partner_rows)
    offsets = jax.random.randint(place_key, (8,), 0, TOKENS // 8)
    rows_hit = TOKENS // 8 * jnp.arange(8) + offsets
    states = states.at[rows_hit].set(strength[:, None] * anchor / anchor_sq)
    return (table, states)


def draw_hidden(key, part):
    return draw_common(key)[1].astype(jnp.bfloat16)


def draw_item_table(key, part):
    return draw_common(key)[0].astype(jnp.bfloat16)


def set_ends(values, stream_key, smallest, top_value):
    longest = values.shape.index(max(values.shape))
    spots = []
    for shift in (0, 1):
        where = [jax.random.randint(jax.random.fold_in(stream_key, axis), (), 0, length) for axis, length in enumerate(values.shape)]
        where[longest] = (where[longest] + shift) % values.shape[longest]
        spots.append(tuple(where))
    return values.at[spots[0]].set(smallest).at[spots[1]].set(top_value)


def wide_ids(rng, dims, number_of, lean):
    loads = [min(1 << octave, number_of + 1 - (1 << octave)) * (1 << 20) // math.isqrt((1 << octave) ** lean) + 1 for octave in range((number_of + 1).bit_length()) if 1 << octave <= number_of]
    scale = 1 + sum(loads) // (1 << 30)
    listing = np.cumsum(np.array([max(1, weight // scale) for weight in loads]))
    lot = jax.random.randint(jax.random.fold_in(rng, 1), dims, 0, int(listing[len(loads) - 1]))
    start = jnp.left_shift(1, jnp.searchsorted(jnp.asarray(listing, jnp.int32), lot, side="right").astype(jnp.int32))
    rank = start - 1 + jax.random.randint(jax.random.fold_in(rng, 4), dims, 0, 1 << 30) % jnp.minimum(start, number_of + 1 - start)
    return jax.random.permutation(jax.random.fold_in(rng, 2), number_of)[rank].astype(jnp.int32)


def split_up(count, total, most, skew):
    weights = [(1 << 20) // math.isqrt(grade ** skew) + 1 for grade in range(2, count + 1)]
    rest, given = total - most - (count - 1), [1] * (count - 1)
    while rest > 0:
        candidates = [i for i in range(count - 1) if given[i] < most]
        mass, left = sum([weights[i] for i in candidates]), rest
        for i in candidates:
            more = min(most - given[i], max(1, left * weights[i] // mass), rest)
            given[i] = given[i] + more
            rest = rest - more
    return np.array([most] + given)


def uneven(key, count, total, bound, slope):
    if count == 2:
        one = jax.random.randint(key, (), max(1, total - bound), min(bound, total - 1) + 1)
        return jnp.stack([one, total - one])
    tallies = jnp.asarray(split_up(count, total, bound, slope), jnp.int32)
    pairs = (count - 1) // 2
    source_of, taker = tallies[1:1 + 2 * pairs:2], tallies[2:2 + 2 * pairs:2]
    margin = jnp.minimum(source_of - 1, bound - taker)
    shifted = jax.random.randint(jax.random.fold_in(key, 1), (pairs,), 0, 1 << 20) % (margin + 1)
    tallies = tallies.at[1:1 + 2 * pairs:2].set(source_of - shifted).at[2:2 + 2 * pairs:2].set(taker + shifted)
    return tallies[jax.random.permutation(jax.random.fold_in(key, 2), count)]


def setup_inputs(seed: int = 0) -> dict:
    streams_of = jax.random.split(jax.random.key(seed), 5)
    return {
        "hidden": draw_hidden(jax.random.fold_in(streams_of[4], 71), 0),
        "item_table": draw_item_table(jax.random.fold_in(streams_of[4], 71), 0),
        "targets": set_ends(wide_ids(streams_of[2], (TOKENS,), ITEMS, 2), jax.random.fold_in(streams_of[2], 3), 0, ITEMS - 1).astype(jnp.int32),
        "lengths": jax.vmap(lambda own: uneven(own, SEQG, TOKG, MAXLEN, 2))(jax.random.split(streams_of[3], N_GRP)).reshape((N_GRP, SEQG)).astype(jnp.int32),
    }


def row_weights(lengths, group_rows):
    seq_count = lengths.shape[1]
    seq_ends = jnp.cumsum(lengths, axis=1)
    starts = seq_ends - lengths
    places = jnp.arange(group_rows, dtype=jnp.int32)
    inside = (places[None, :, None] >= starts[:, None, :]) & (places[None, :, None] < seq_ends[:, None, :])
    row_length = jnp.sum(jnp.where(inside, lengths[:, None, :].astype(jnp.float32), jnp.float32(0.0)), axis=2)
    return ((group_rows / seq_count) / row_length).reshape(-1)


def reference(hidden, item_table, targets, lengths):
    token_count = hidden.shape[0]
    group_rows = token_count // lengths.shape[0]
    states = hidden.astype(jnp.float32)
    block_count = ITEMS // ITEM_DEV
    blocks = item_table.reshape(block_count, ITEM_DEV, D)
    block_starts = ITEM_DEV * jnp.arange(block_count, dtype=jnp.int32)

    def visit(carried, block_pair):
        highest, running, picked = carried
        item_block, block_start = block_pair
        scores = jnp.dot(states, item_block.astype(jnp.float32).T, precision=lax.Precision.HIGHEST)
        new_max = jnp.maximum(highest, jnp.max(scores, axis=1))
        running = running * jnp.exp(highest - new_max) + jnp.sum(jnp.exp(scores - new_max[:, None]), axis=1)
        columns = block_start + jnp.arange(ITEM_DEV, dtype=jnp.int32)
        matched = targets[:, None] == columns[None, :]
        picked = picked + jnp.sum(jnp.where(matched, scores, jnp.float32(0.0)), axis=1)
        return (new_max, running, picked), None

    start_stats = (jnp.full((token_count,), -jnp.inf, dtype=jnp.float32),
                   jnp.zeros((token_count,), jnp.float32), jnp.zeros((token_count,), jnp.float32))
    final_stats, unused = lax.scan(visit, start_stats, (blocks, block_starts))
    row_max, exp_total, target_score = final_stats
    log_total = row_max + jnp.log(exp_total)
    row_loss = log_total - target_score
    weight = row_weights(lengths, group_rows)

    def back_visit(state_grad, block_pair):
        item_block, block_start = block_pair
        block_f = item_block.astype(jnp.float32)
        scores = jnp.dot(states, block_f.T, precision=lax.Precision.HIGHEST)
        columns = block_start + jnp.arange(ITEM_DEV, dtype=jnp.int32)
        matched = (targets[:, None] == columns[None, :]).astype(jnp.float32)
        signal = (weight[:, None] * (jnp.exp(scores - log_total[:, None]) - matched)).astype(jnp.bfloat16)
        signal_f = signal.astype(jnp.float32)
        state_grad = state_grad + jnp.dot(signal_f, block_f, precision=lax.Precision.HIGHEST)
        item_grad = jnp.dot(signal_f.T, states, precision=lax.Precision.HIGHEST)
        return state_grad, item_grad.astype(jnp.bfloat16)

    state_grad, item_grads = lax.scan(back_visit, jnp.zeros((token_count, D), jnp.float32), (blocks, block_starts))
    return row_loss, state_grad.astype(jnp.bfloat16), item_grads.reshape(ITEMS, D)
```

```python
import functools
import jax
import jax.numpy as jnp
from jax import lax
from jax.experimental import pallas as pl
from jax.experimental.pallas import tpu as pltpu
from jax.sharding import PartitionSpec as P


def block_width():
    return 2048


def weights_for(lengths, group_index, group_rows):
    seq_count = lengths.shape[1]
    own_lengths = lax.dynamic_index_in_dim(lengths, group_index, 0, keepdims=False)
    seq_ends = jnp.cumsum(own_lengths)
    starts = seq_ends - own_lengths
    places = jnp.arange(group_rows, dtype=jnp.int32)
    inside = (places[:, None] >= starts[None, :]) & (places[:, None] < seq_ends[None, :])
    row_length = jnp.sum(
        jnp.where(inside, own_lengths[None, :].astype(jnp.float32), jnp.float32(0.0)), axis=1
    )
    return group_rows / seq_count / row_length


def split_blocks(item_table, first_item, block_size):
    block_count = item_table.shape[0] // block_size
    blocks = item_table.reshape(block_count, block_size, item_table.shape[1])
    block_starts = first_item + block_size * jnp.arange(block_count, dtype=jnp.int32)
    return (blocks, block_starts)


def partial_stats(states, target_ids, item_table, first_item, block_size):
    blocks, block_starts = split_blocks(item_table, first_item, block_size)
    row_count = states.shape[0]

    def partial_visit(carried, block_pair):
        highest, running, picked = carried
        item_block, block_start = block_pair
        scores = jnp.einsum("rd,id->ri", states, item_block, preferred_element_type=jnp.float32)
        new_max = jnp.maximum(highest, jnp.max(scores, axis=1))
        running = running * jnp.exp(highest - new_max) + jnp.sum(
            jnp.exp(scores - new_max[:, None]), axis=1
        )
        columns = block_start + jnp.arange(block_size, dtype=jnp.int32)
        matched = target_ids[:, None] == columns[None, :]
        picked = picked + jnp.sum(jnp.where(matched, scores, jnp.float32(0.0)), axis=1)
        return ((new_max, running, picked), None)

    start_stats = (
        jnp.full((row_count,), -jnp.inf, dtype=jnp.float32),
        jnp.zeros((row_count,), jnp.float32),
        jnp.zeros((row_count,), jnp.float32),
    )
    final_stats, unused = lax.scan(partial_visit, start_stats, (blocks, block_starts))
    return final_stats


def backward(states, target_ids, item_table, first_item, block_size, log_total, row_weight):
    blocks, block_starts = split_blocks(item_table, first_item, block_size)

    def backward_visit(state_grad, block_pair):
        item_block, block_start = block_pair
        scores = jnp.einsum("rd,id->ri", states, item_block, preferred_element_type=jnp.float32)
        columns = block_start + jnp.arange(block_size, dtype=jnp.int32)
        matched = (target_ids[:, None] == columns[None, :]).astype(jnp.float32)
        signal = (row_weight[:, None] * (jnp.exp(scores - log_total[:, None]) - matched)).astype(
            jnp.bfloat16
        )
        state_grad = state_grad + jnp.dot(signal, item_block, preferred_element_type=jnp.float32)
        item_grad = jnp.einsum("ri,rd->id", signal, states, preferred_element_type=jnp.float32)
        return (state_grad, item_grad)

    start_grad = jnp.zeros((states.shape[0], states.shape[1]), jnp.float32)
    state_grad, item_grads = lax.scan(backward_visit, start_grad, (blocks, block_starts))
    return (state_grad, item_grads.reshape(item_table.shape[0], item_table.shape[1]))


def local(hidden, item_table, targets, lengths):
    rows_local = hidden.shape[0]
    items_local = item_table.shape[0]
    block_size = block_width()
    item_rank = lax.axis_index("item")
    group_rank = lax.axis_index("grp")
    first_item = item_rank * items_local
    group_states, group_targets = (
        lax.all_gather(hidden, "item", axis=0, tiled=True),
        lax.all_gather(targets, "item", axis=0, tiled=True),
    )
    group_rows = group_states.shape[0]
    states, target_ids = (
        lax.all_gather(group_states, "grp", axis=0, tiled=True),
        lax.all_gather(group_targets, "grp", axis=0, tiled=True),
    )
    row_weight = jnp.concatenate(
        [weights_for(lengths, member, group_rows) for member in range(lengths.shape[0])]
    )
    own_start = group_rank * group_rows + item_rank * rows_local
    highest, running, picked = partial_stats(states, target_ids, item_table, first_item, block_size)
    row_max = lax.pmax(highest, "item")
    exp_total, target_score = lax.psum((running * jnp.exp(highest - row_max), picked), "item")
    log_total = row_max + jnp.log(exp_total)
    losses = log_total - target_score
    row_loss = lax.dynamic_slice_in_dim(losses, own_start, rows_local)
    half_items = items_local // 2
    own_items = lax.dynamic_slice_in_dim(item_table, group_rank * half_items, half_items)
    state_grad, table_grad = backward(
        states,
        target_ids,
        own_items,
        first_item + group_rank * half_items,
        block_width(),
        log_total,
        row_weight,
    )
    group_grad = lax.psum_scatter(state_grad, "grp", scatter_dimension=0, tiled=True)
    hidden_grad = lax.psum_scatter(group_grad, "item", scatter_dimension=0, tiled=True)
    return (row_loss, hidden_grad.astype(jnp.bfloat16), table_grad.astype(jnp.bfloat16))


def fused_kernel(
    item_size,
    group_size,
    chunk,
    hidden_ref,
    targets_ref,
    lengths_ref,
    table_ref,
    loss_ref,
    hgrad_ref,
    tgrad_ref,
    target_pad,
    gathered,
    states,
    items,
    items_t,
    probs,
    signal,
    chunk_max,
    own_stats,
    mate_stats,
    all_stats,
    grad_t,
    grads,
    mate_grads,
    send_grads,
    recv_grads,
    stage,
    items_sem,
    out_sems,
    gather_send,
    gather_recv,
    relay_send,
    relay_recv,
    stat_mate_sems,
    stat_send,
    stat_recv,
    grad_mate_sems,
    grad_send,
    grad_recv,
):
    rows, width = hidden_ref.shape
    half = items.shape[0]
    chunk_count = half // chunk
    padded = gathered.shape[1]
    positions = states.shape[0]
    chips_per_group = item_size // 2
    chips = chips_per_group * group_size
    group_rows = rows * item_size

    item_rank = lax.axis_index("item")
    group_rank = lax.axis_index("grp")
    core = lax.rem(item_rank, 2)
    chip = group_rank * chips_per_group + item_rank // 2
    own_block = group_rank * item_size + item_rank
    first_item = (item_rank * group_size + group_rank) * half

    def chip_device(which, core_index):
        return {
            "item": 2 * lax.rem(which, chips_per_group) + core_index,
            "grp": which // chips_per_group,
        }

    def block_of(which, core_index):
        return (
            (which // chips_per_group) * item_size
            + 2 * lax.rem(which, chips_per_group)
            + core_index
        )

    mate = {"item": 2 * (item_rank // 2) + 1 - core, "grp": group_rank}

    def remote(src, dst, send_sem, recv_sem, device):
        return pltpu.make_async_remote_copy(
            src_ref=src,
            dst_ref=dst,
            send_sem=send_sem,
            recv_sem=recv_sem,
            device_id=device,
            device_id_type=pl.DeviceIdType.MESH,
        )

    def each_peer(body):
        def step(offset, carried):
            body(lax.rem(chip + offset, chips))
            return carried

        lax.fori_loop(1, chips, step, 0)

    def each_source(body):
        def step(offset, carried):
            body(lax.rem(chip + chips - offset, chips))
            return carried

        lax.fori_loop(1, chips, step, 0)

    items_copy = pltpu.make_async_copy(
        table_ref.at[pl.ds(pl.multiple_of(group_rank * half, chunk), half)], items, items_sem
    )
    items_copy.start()

    barrier = pltpu.get_barrier_semaphore()
    pl.semaphore_signal(barrier, inc=1, device_id=mate, device_id_type=pl.DeviceIdType.MESH)
    each_peer(
        lambda peer: pl.semaphore_signal(
            barrier,
            inc=1,
            device_id=chip_device(peer, core),
            device_id_type=pl.DeviceIdType.MESH,
        )
    )

    target_pad[...] = jnp.zeros_like(target_pad)
    target_pad[0:1, 0:rows] = targets_ref[...]
    wide_targets = jnp.broadcast_to(target_pad[0:1, :], (8, width))
    digit_row = lax.broadcasted_iota(jnp.int32, (8, width), 0)
    digits = jnp.where(
        digit_row == 0,
        wide_targets & 255,
        jnp.where(
            digit_row == 1,
            (wide_targets >> 8) & 255,
            jnp.where(digit_row == 2, (wide_targets >> 16) & 255, 0),
        ),
    ).astype(jnp.float32)
    gathered[own_block] = jnp.concatenate(
        [hidden_ref[...].astype(jnp.float32), digits], axis=0
    ).astype(jnp.bfloat16)

    pl.semaphore_wait(barrier, chips)

    def gather_copy(peer):
        return remote(
            gathered.at[own_block],
            gathered.at[own_block],
            gather_send.at[peer],
            gather_recv.at[chip],
            chip_device(peer, core),
        )

    def gather_arrival(source):
        block = gathered.at[block_of(source, core)]
        return remote(
            block, block, gather_send.at[source], gather_recv.at[source], chip_device(source, core)
        )

    def relay_copy(source):
        block = gathered.at[block_of(source, core)]
        return remote(block, block, relay_send.at[source], relay_recv.at[source], mate)

    def relay_arrival(source):
        block = gathered.at[block_of(source, 1 - core)]
        return remote(block, block, relay_send.at[source], relay_recv.at[source], mate)

    each_peer(lambda peer: gather_copy(peer).start())
    relay_copy(chip).start()

    places = lax.broadcasted_iota(jnp.int32, (1, positions), 1)
    row_length = jnp.zeros((1, positions), jnp.float32)
    for member in range(group_size):
        start = member * group_rows
        for seq in range(lengths_ref.shape[1]):
            length = lengths_ref[member, seq]
            inside = (places >= start) & (places < start + length)
            row_length = jnp.where(inside, length.astype(jnp.float32), row_length)
            start = start + length
    weight = (group_rows / lengths_ref.shape[1]) / row_length

    items_copy.wait()
    for index in range(chunk_count):
        span = pl.ds(index * chunk, chunk)
        items_t[:, span] = items[span, :].astype(jnp.float32).T.astype(jnp.bfloat16)

    def pass_on(source):
        gather_arrival(source).wait_recv()
        relay_copy(source).start()

    each_source(pass_on)
    relay_arrival(chip).wait_recv()
    each_source(lambda source: relay_arrival(source).wait_recv())

    everything = gathered[...].astype(jnp.float32)
    states[...] = everything[:, :rows, :].reshape(positions, width).astype(jnp.bfloat16)
    lanes = 128
    code = everything[:, rows:padded, :lanes]
    code_rows = code.shape[0] * code.shape[1]
    code = code.reshape(code_rows, lanes).astype(jnp.bfloat16)
    lane_index = lax.broadcasted_iota(jnp.int32, (lanes, positions), 0)
    place_index = lax.broadcasted_iota(jnp.int32, (lanes, positions), 1)
    spread = (lax.rem(place_index, rows) == lane_index).astype(jnp.float32).astype(jnp.bfloat16)
    coded = jnp.dot(code, spread, preferred_element_type=jnp.float32)
    code_index = lax.broadcasted_iota(jnp.int32, (code_rows, positions), 0)
    code_place = lax.broadcasted_iota(jnp.int32, (code_rows, positions), 1)
    digit = lax.rem(code_index, 8)
    scale = jnp.where(
        digit == 0,
        jnp.float32(1.0),
        jnp.where(
            digit == 1,
            jnp.float32(256.0),
            jnp.where(digit == 2, jnp.float32(65536.0), jnp.float32(0.0)),
        ),
    )
    target_ids = jnp.sum(
        jnp.where(code_index // 8 == code_place // rows, coded * scale, 0.0),
        axis=0,
        keepdims=True,
    ).astype(jnp.int32)
    local_target = target_ids - first_item

    def forward(index, carried):
        highest, running, picked = carried
        base = pl.multiple_of(index * chunk, chunk)
        scores = lax.dot_general(
            items[pl.ds(base, chunk), :],
            states[...],
            (((1,), (1,)), ((), ())),
            preferred_element_type=jnp.float32,
        )
        top = jnp.max(scores, axis=0, keepdims=True)
        exps = jnp.exp(scores - top)
        probs[pl.ds(base, chunk), :] = exps
        chunk_max[index] = top
        total = jnp.sum(exps, axis=0, keepdims=True)
        item_index = lax.broadcasted_iota(jnp.int32, (chunk, positions), 0)
        matched = item_index == local_target - base
        picked = picked + jnp.sum(jnp.where(matched, scores, 0.0), axis=0, keepdims=True)
        new_max = jnp.maximum(highest, top)
        running = running * jnp.exp(highest - new_max) + total * jnp.exp(top - new_max)
        return (new_max, running, picked)

    zero_row = jnp.zeros((1, positions), jnp.float32)
    highest, running, picked = lax.fori_loop(
        0,
        chunk_count,
        forward,
        (jnp.full((1, positions), -jnp.inf, jnp.float32), zero_row, zero_row),
    )
    own_stats[0:1, :] = highest + jnp.log(running)
    own_stats[1:2, :] = picked

    stat_mate = remote(
        own_stats, mate_stats, stat_mate_sems.at[0], stat_mate_sems.at[1], mate
    )
    stat_mate.start()
    stat_mate.wait()

    def log_add(a, b):
        top = jnp.maximum(a, b)
        return top + jnp.log(jnp.exp(a - top) + jnp.exp(b - top))

    all_stats[chip] = jnp.concatenate(
        [
            log_add(own_stats[0:1, :], mate_stats[0:1, :]),
            own_stats[1:2, :] + mate_stats[1:2, :],
        ],
        axis=0,
    )

    def stat_copy(peer):
        return remote(
            all_stats.at[chip],
            all_stats.at[chip],
            stat_send.at[peer],
            stat_recv.at[chip],
            chip_device(peer, core),
        )

    def stat_arrival(source):
        return remote(
            all_stats.at[source],
            all_stats.at[source],
            stat_send.at[source],
            stat_recv.at[source],
            chip_device(source, core),
        )

    each_peer(lambda peer: stat_copy(peer).start())
    each_source(lambda source: stat_arrival(source).wait_recv())

    row_max = all_stats[0, 0:1, :]
    for index in range(1, chips):
        row_max = jnp.maximum(row_max, all_stats[index, 0:1, :])
    exp_total = zero_row
    target_score = zero_row
    for index in range(chips):
        exp_total = exp_total + jnp.exp(all_stats[index, 0:1, :] - row_max)
        target_score = target_score + all_stats[index, 1:2, :]
    log_total = row_max + jnp.log(exp_total)

    losses = jnp.broadcast_to(log_total - target_score, (rows, positions))
    row_index = lax.broadcasted_iota(jnp.int32, (rows, positions), 0)
    row_place = lax.broadcasted_iota(jnp.int32, (rows, positions), 1)
    own_losses = jnp.sum(
        jnp.where(row_place == row_index + own_block * rows, losses, 0.0), axis=1, keepdims=True
    )
    cell_row = lax.broadcasted_iota(jnp.int32, (rows, lanes), 0)
    cell_lane = lax.broadcasted_iota(jnp.int32, (rows, lanes), 1)
    loss_row = jnp.sum(
        jnp.where(cell_row == cell_lane, jnp.broadcast_to(own_losses, (rows, lanes)), 0.0),
        axis=0,
        keepdims=True,
    )
    loss_ref[...] = loss_row[:, :rows]

    grad_t[...] = jnp.zeros_like(grad_t)

    def backward_states(index, carried):
        base = pl.multiple_of(index * chunk, chunk)
        factor = weight * jnp.exp(chunk_max[index] - log_total)
        item_index = lax.broadcasted_iota(jnp.int32, (chunk, positions), 0)
        matched = item_index == local_target - base
        part = probs[pl.ds(base, chunk), :] * factor - jnp.where(
            matched, jnp.broadcast_to(weight, (chunk, positions)), 0.0
        )
        part = part.astype(jnp.bfloat16)
        signal[pl.ds(base, chunk), :] = part
        grad_t[...] += jnp.dot(
            items_t[:, pl.ds(base, chunk)], part, preferred_element_type=jnp.float32
        )
        return carried

    lax.fori_loop(0, chunk_count, backward_states, 0)

    turned = grad_t[...].T
    for group in range(group_size):
        for rank in range(item_size):
            start = (group * item_size + rank) * rows
            grads[rank % 2, group * chips_per_group + rank // 2] = turned[start : start + rows, :]

    grad_mate = remote(
        grads.at[1 - core], mate_grads, grad_mate_sems.at[0], grad_mate_sems.at[1], mate
    )
    grad_mate.start()

    def out_copy(index):
        span = pl.ds(pl.multiple_of(index * chunk, chunk), chunk)
        return pltpu.make_async_copy(stage.at[span], tgrad_ref.at[span], out_sems.at[index])

    def backward_items(index, carried):
        base = pl.multiple_of(index * chunk, chunk)
        stage[pl.ds(base, chunk), :] = jnp.dot(
            signal[pl.ds(base, chunk), :], states[...], preferred_element_type=jnp.float32
        ).astype(jnp.bfloat16)
        out_copy(index).start()
        return carried

    early = chunk_count // 2
    lax.fori_loop(0, early, backward_items, 0)

    grad_mate.wait()
    send_grads[...] = (grads[core] + mate_grads[...]).astype(send_grads.dtype)

    def grad_copy(peer):
        return remote(
            send_grads.at[peer],
            recv_grads.at[chip],
            grad_send.at[peer],
            grad_recv.at[chip],
            chip_device(peer, core),
        )

    def grad_arrival(source):
        return remote(
            send_grads.at[source],
            recv_grads.at[source],
            grad_send.at[source],
            grad_recv.at[source],
            chip_device(source, core),
        )

    each_peer(lambda peer: grad_copy(peer).start())
    recv_grads[chip] = send_grads[chip]

    lax.fori_loop(early, chunk_count, backward_items, 0)

    each_source(lambda source: grad_arrival(source).wait_recv())
    total = recv_grads[0].astype(jnp.float32)
    for index in range(1, chips):
        total = total + recv_grads[index].astype(jnp.float32)
    hgrad_ref[...] = total.astype(jnp.bfloat16)

    relay_copy(chip).wait_send()

    def finish(peer):
        gather_copy(peer).wait_send()
        relay_copy(peer).wait_send()
        stat_copy(peer).wait_send()
        grad_copy(peer).wait_send()

    each_peer(finish)

    def drain(index, carried):
        out_copy(index).wait()
        return carried

    lax.fori_loop(0, chunk_count, drain, 0)


def fused(item_size, group_size, chunk, wire, hidden, item_table, targets, lengths):
    rows, width = hidden.shape
    half = item_table.shape[0] // group_size
    positions = rows * item_size * group_size
    chips = item_size * group_size // 2
    chunk_count = half // chunk
    padded = rows + 8
    vmem = pl.BlockSpec(memory_space=pltpu.VMEM)
    dma = pltpu.SemaphoreType.DMA
    f32, bf16 = jnp.float32, jnp.bfloat16
    loss, hgrad, tgrad = pl.pallas_call(
        functools.partial(fused_kernel, item_size, group_size, chunk),
        out_shape=(
            jax.ShapeDtypeStruct((1, rows), f32),
            jax.ShapeDtypeStruct((rows, width), bf16),
            jax.ShapeDtypeStruct((half, width), bf16),
        ),
        in_specs=[
            vmem,
            vmem,
            pl.BlockSpec(memory_space=pltpu.SMEM),
            pl.BlockSpec(memory_space=pl.ANY),
        ],
        out_specs=(vmem, vmem, pl.BlockSpec(memory_space=pl.ANY)),
        scratch_shapes=[
            pltpu.VMEM((8, width), jnp.int32),
            pltpu.VMEM((2 * chips, padded, width), bf16),
            pltpu.VMEM((positions, width), bf16),
            pltpu.VMEM((half, width), bf16),
            pltpu.VMEM((width, half), bf16),
            pltpu.VMEM((half, positions), f32),
            pltpu.VMEM((half, positions), bf16),
            pltpu.VMEM((chunk_count, 1, positions), f32),
            pltpu.VMEM((2, positions), f32),
            pltpu.VMEM((2, positions), f32),
            pltpu.VMEM((chips, 2, positions), f32),
            pltpu.VMEM((width, positions), f32),
            pltpu.VMEM((2, chips, rows, width), f32),
            pltpu.VMEM((chips, rows, width), f32),
            pltpu.VMEM((chips, rows, width), wire),
            pltpu.VMEM((chips, rows, width), wire),
            pltpu.VMEM((half, width), bf16),
            dma,
            dma((chunk_count,)),
            dma((chips,)),
            dma((chips,)),
            dma((chips,)),
            dma((chips,)),
            dma((2,)),
            dma((chips,)),
            dma((chips,)),
            dma((2,)),
            dma((chips,)),
            dma((chips,)),
        ],
        compiler_params=pltpu.CompilerParams(
            collective_id=0, has_side_effects=True, vmem_limit_bytes=60 * 1024 * 1024
        ),
        name="fused_loss",
    )(hidden, targets.reshape(1, rows), lengths, item_table)
    return loss.reshape(rows), hgrad, tgrad


def solution(mesh):
    in_specs = (P(("grp", "item"), None), P("item", None), P(("grp", "item")), P())
    out_specs = (P(("grp", "item")), P(("grp", "item"), None), P(("item", "grp"), None))
    item_size, group_size = mesh.shape["item"], mesh.shape["grp"]

    def body(hidden, item_table, targets, lengths):
        rows, width = hidden.shape
        half = item_table.shape[0] // group_size
        chunk = min(512, half)
        fits = (
            rows % 8 == 0
            and rows <= 128
            and width % 128 == 0
            and item_size % 2 == 0
            and half * group_size == item_table.shape[0]
            and half % chunk == 0
            and chunk % 128 == 0
            and (rows * item_size * group_size) % 128 == 0
            and item_size * item_table.shape[0] <= 1 << 24
        )
        if fits:
            return fused(
                item_size, group_size, chunk, jnp.float32, hidden, item_table, targets, lengths
            )
        return local(hidden, item_table, targets, lengths)

    return jax.shard_map(body, mesh=mesh, in_specs=in_specs, out_specs=out_specs, check_vma=False)
```

```python
import functools
import jax
import jax.numpy as jnp
from jax import lax
from jax.experimental import pallas as pl
from jax.experimental.pallas import tpu as pltpu
from jax.sharding import PartitionSpec as P


def block_width():
    return 2048


def weights_for(lengths, group_index, group_rows):
    seq_count = lengths.shape[1]
    own_lengths = lax.dynamic_index_in_dim(lengths, group_index, 0, keepdims=False)
    seq_ends = jnp.cumsum(own_lengths)
    starts = seq_ends - own_lengths
    places = jnp.arange(group_rows, dtype=jnp.int32)
    inside = (places[:, None] >= starts[None, :]) & (places[:, None] < seq_ends[None, :])
    row_length = jnp.sum(
        jnp.where(inside, own_lengths[None, :].astype(jnp.float32), jnp.float32(0.0)), axis=1
    )
    return group_rows / seq_count / row_length


def split_blocks(item_table, first_item, block_size):
    block_count = item_table.shape[0] // block_size
    blocks = item_table.reshape(block_count, block_size, item_table.shape[1])
    block_starts = first_item + block_size * jnp.arange(block_count, dtype=jnp.int32)
    return (blocks, block_starts)


def partial_stats(states, target_ids, item_table, first_item, block_size):
    blocks, block_starts = split_blocks(item_table, first_item, block_size)
    row_count = states.shape[0]

    def partial_visit(carried, block_pair):
        highest, running, picked = carried
        item_block, block_start = block_pair
        scores = jnp.einsum("rd,id->ri", states, item_block, preferred_element_type=jnp.float32)
        new_max = jnp.maximum(highest, jnp.max(scores, axis=1))
        running = running * jnp.exp(highest - new_max) + jnp.sum(
            jnp.exp(scores - new_max[:, None]), axis=1
        )
        columns = block_start + jnp.arange(block_size, dtype=jnp.int32)
        matched = target_ids[:, None] == columns[None, :]
        picked = picked + jnp.sum(jnp.where(matched, scores, jnp.float32(0.0)), axis=1)
        return ((new_max, running, picked), None)

    start_stats = (
        jnp.full((row_count,), -jnp.inf, dtype=jnp.float32),
        jnp.zeros((row_count,), jnp.float32),
        jnp.zeros((row_count,), jnp.float32),
    )
    final_stats, unused = lax.scan(partial_visit, start_stats, (blocks, block_starts))
    return final_stats


def backward(states, target_ids, item_table, first_item, block_size, log_total, row_weight):
    blocks, block_starts = split_blocks(item_table, first_item, block_size)

    def backward_visit(state_grad, block_pair):
        item_block, block_start = block_pair
        scores = jnp.einsum("rd,id->ri", states, item_block, preferred_element_type=jnp.float32)
        columns = block_start + jnp.arange(block_size, dtype=jnp.int32)
        matched = (target_ids[:, None] == columns[None, :]).astype(jnp.float32)
        signal = (row_weight[:, None] * (jnp.exp(scores - log_total[:, None]) - matched)).astype(
            jnp.bfloat16
        )
        state_grad = state_grad + jnp.dot(signal, item_block, preferred_element_type=jnp.float32)
        item_grad = jnp.einsum("ri,rd->id", signal, states, preferred_element_type=jnp.float32)
        return (state_grad, item_grad)

    start_grad = jnp.zeros((states.shape[0], states.shape[1]), jnp.float32)
    state_grad, item_grads = lax.scan(backward_visit, start_grad, (blocks, block_starts))
    return (state_grad, item_grads.reshape(item_table.shape[0], item_table.shape[1]))


def local(hidden, item_table, targets, lengths):
    rows_local = hidden.shape[0]
    items_local = item_table.shape[0]
    block_size = block_width()
    item_rank = lax.axis_index("item")
    group_rank = lax.axis_index("grp")
    first_item = item_rank * items_local
    group_states, group_targets = (
        lax.all_gather(hidden, "item", axis=0, tiled=True),
        lax.all_gather(targets, "item", axis=0, tiled=True),
    )
    group_rows = group_states.shape[0]
    states, target_ids = (
        lax.all_gather(group_states, "grp", axis=0, tiled=True),
        lax.all_gather(group_targets, "grp", axis=0, tiled=True),
    )
    row_weight = jnp.concatenate(
        [weights_for(lengths, member, group_rows) for member in range(lengths.shape[0])]
    )
    own_start = group_rank * group_rows + item_rank * rows_local
    highest, running, picked = partial_stats(states, target_ids, item_table, first_item, block_size)
    row_max = lax.pmax(highest, "item")
    exp_total, target_score = lax.psum((running * jnp.exp(highest - row_max), picked), "item")
    log_total = row_max + jnp.log(exp_total)
    losses = log_total - target_score
    row_loss = lax.dynamic_slice_in_dim(losses, own_start, rows_local)
    half_items = items_local // 2
    own_items = lax.dynamic_slice_in_dim(item_table, group_rank * half_items, half_items)
    state_grad, table_grad = backward(
        states,
        target_ids,
        own_items,
        first_item + group_rank * half_items,
        block_width(),
        log_total,
        row_weight,
    )
    group_grad = lax.psum_scatter(state_grad, "grp", scatter_dimension=0, tiled=True)
    hidden_grad = lax.psum_scatter(group_grad, "item", scatter_dimension=0, tiled=True)
    return (row_loss, hidden_grad.astype(jnp.bfloat16), table_grad.astype(jnp.bfloat16))


def fused_kernel(
    item_size,
    group_size,
    near_size,
    chunk,
    hidden_ref,
    targets_ref,
    lengths_ref,
    table_ref,
    loss_ref,
    hgrad_ref,
    tgrad_ref,
    target_pad,
    gathered,
    states,
    items,
    items_t,
    probs,
    signal,
    chunk_max,
    own_stats,
    mate_stats,
    all_stats,
    grad_t,
    grads,
    mate_grads,
    send_grads,
    wire_grads,
    recv_grads,
    stage,
    items_sem,
    out_sems,
    gather_send,
    gather_recv,
    relay_send,
    relay_recv,
    stat_mate_send,
    stat_mate_recv,
    stat_send,
    stat_recv,
    grad_mate_sems,
    grad_send,
    grad_recv,
):
    rows, width = hidden_ref.shape
    half = items.shape[0]
    chunk_count = half // chunk
    padded = gathered.shape[2]
    slots = states.shape[1]
    positions = 2 * slots
    chips_per_group = item_size // 2
    chips = chips_per_group * group_size
    far_size = chips_per_group // near_size
    group_rows = rows * item_size
    lanes = 128

    item_rank = lax.axis_index("item")
    group_rank = lax.axis_index("grp")
    core = lax.rem(item_rank, 2)
    in_group = item_rank // 2
    chip = group_rank * chips_per_group + in_group
    near = lax.rem(in_group, near_size)
    far = in_group // near_size
    first_item = (item_rank * group_size + group_rank) * half

    def chip_device(which):
        return {
            "item": 2 * lax.rem(which, chips_per_group) + core,
            "grp": which // chips_per_group,
        }

    mate = {"item": 2 * in_group + 1 - core, "grp": group_rank}

    def remote(src, dst, send_sem, recv_sem, device):
        return pltpu.make_async_remote_copy(
            src_ref=src,
            dst_ref=dst,
            send_sem=send_sem,
            recv_sem=recv_sem,
            device_id=device,
            device_id_type=pl.DeviceIdType.MESH,
        )

    def each_peer(body):
        def step(offset, carried):
            body(lax.rem(chip + offset, chips))
            return carried

        lax.fori_loop(1, chips, step, 0)

    def flipped(offset):
        place = far
        for bit in range(offset.bit_length()):
            size = 1 << bit
            if offset & size:
                place = place + size - 2 * size * lax.rem(far // size, 2)
        return place

    far_places = [flipped(offset) for offset in range(far_size)]
    columns = [
        (lax.rem(near + step_near, near_size), lax.rem(group_rank + step_group, group_size))
        for step_near in range(near_size)
        for step_group in range(group_size)
    ]

    def chip_at(column, place):
        return column[1] * chips_per_group + place * near_size + column[0]

    far_chips = [chip_at(columns[0], place) for place in far_places[1:]]
    near_chips = [chip_at(column, far) for column in columns[1:]]

    items_copy = pltpu.make_async_copy(
        table_ref.at[pl.ds(pl.multiple_of(group_rank * half, chunk), half)], items, items_sem
    )
    items_copy.start()

    barrier = pltpu.get_barrier_semaphore()
    greeted = [mate] + [chip_device(peer) for peer in far_chips + near_chips]
    for device in greeted:
        pl.semaphore_signal(
            barrier, inc=1, device_id=device, device_id_type=pl.DeviceIdType.MESH
        )

    target_pad[...] = jnp.zeros_like(target_pad)
    target_pad[0:1, 0:rows] = targets_ref[...]
    wide_targets = jnp.broadcast_to(target_pad[0:1, :], (8, width))
    digit_row = lax.broadcasted_iota(jnp.int32, (8, width), 0)
    digits = jnp.where(
        digit_row == 0,
        wide_targets & 255,
        jnp.where(
            digit_row == 1,
            (wide_targets >> 8) & 255,
            jnp.where(digit_row == 2, (wide_targets >> 16) & 255, 0),
        ),
    ).astype(jnp.float32)
    gathered[core, chip] = jnp.concatenate(
        [hidden_ref[...].astype(jnp.float32), digits], axis=0
    ).astype(jnp.bfloat16)

    pl.semaphore_wait(barrier, len(greeted))

    def gather_copy(source, lane, peer):
        block = gathered.at[core, source]
        return remote(
            block, block, gather_send.at[lane], gather_recv.at[source], chip_device(peer)
        )

    def relay_copy(source):
        block = gathered.at[core, source]
        return remote(block, block, relay_send.at[source], relay_recv.at[source], mate)

    def relay_arrival(source):
        block = gathered.at[1 - core, source]
        return remote(block, block, relay_send.at[source], relay_recv.at[source], mate)

    sent = []

    def send_on(source, peers):
        for peer in peers:
            copy = gather_copy(source, len(sent), peer)
            copy.start()
            sent.append(copy)

    send_on(chip, far_chips)
    send_on(chip, near_chips)
    relay_copy(chip).start()

    slot_index = lax.broadcasted_iota(jnp.int32, (1, positions), 1)
    slot_block = slot_index // rows
    slot_chip = lax.rem(slot_block, chips)
    places = (
        (slot_chip // chips_per_group) * item_size
        + 2 * lax.rem(slot_chip, chips_per_group)
        + slot_block // chips
    ) * rows + lax.rem(slot_index, rows)
    row_length = jnp.zeros((1, positions), jnp.float32)
    for member in range(group_size):
        start = member * group_rows
        for seq in range(lengths_ref.shape[1]):
            length = lengths_ref[member, seq]
            inside = (places >= start) & (places < start + length)
            row_length = jnp.where(inside, length.astype(jnp.float32), row_length)
            start = start + length
    weight = (group_rows / lengths_ref.shape[1]) / row_length

    items_copy.wait()
    for index in range(chunk_count):
        span = pl.ds(index * chunk, chunk)
        items_t[:, span] = items[span, :].astype(jnp.float32).T.astype(jnp.bfloat16)

    for source in far_chips:
        gather_copy(source, 0, source).wait_recv()
        send_on(source, near_chips)
        relay_copy(source).start()
    others = [chip_at(column, place) for place in far_places for column in columns[1:]]
    for source in others:
        gather_copy(source, 0, source).wait_recv()
        relay_copy(source).start()
    all_chips = [chip] + far_chips + others
    for source in all_chips:
        relay_arrival(source).wait_recv()

    everything = gathered[...].reshape(2 * chips, padded, width).astype(jnp.float32)
    states[...] = (
        everything[:, :rows, :].reshape(2, slots, width).astype(jnp.bfloat16)
    )
    code = everything[:, rows:padded, :lanes]
    code_rows = code.shape[0] * code.shape[1]
    code = code.reshape(code_rows, lanes).astype(jnp.bfloat16)
    lane_index = lax.broadcasted_iota(jnp.int32, (lanes, positions), 0)
    place_index = lax.broadcasted_iota(jnp.int32, (lanes, positions), 1)
    spread = (lax.rem(place_index, rows) == lane_index).astype(jnp.float32).astype(jnp.bfloat16)
    coded = jnp.dot(code, spread, preferred_element_type=jnp.float32)
    code_index = lax.broadcasted_iota(jnp.int32, (code_rows, positions), 0)
    code_place = lax.broadcasted_iota(jnp.int32, (code_rows, positions), 1)
    digit = lax.rem(code_index, 8)
    scale = jnp.where(
        digit == 0,
        jnp.float32(1.0),
        jnp.where(
            digit == 1,
            jnp.float32(256.0),
            jnp.where(digit == 2, jnp.float32(65536.0), jnp.float32(0.0)),
        ),
    )
    target_ids = jnp.sum(
        jnp.where(code_index // 8 == code_place // rows, coded * scale, 0.0),
        axis=0,
        keepdims=True,
    ).astype(jnp.int32)
    local_target = target_ids - first_item

    def part_of(row, part):
        return row[:, part * slots : (part + 1) * slots]

    def forward(part):
        wanted = part_of(local_target, part)

        def visit(index, carried):
            highest, running, picked = carried
            base = pl.multiple_of(index * chunk, chunk)
            scores = lax.dot_general(
                items[pl.ds(base, chunk), :],
                states[part],
                (((1,), (1,)), ((), ())),
                preferred_element_type=jnp.float32,
            )
            top = jnp.max(scores, axis=0, keepdims=True)
            exps = jnp.exp(scores - top)
            probs[part, pl.ds(base, chunk), :] = exps
            chunk_max[part, index] = top
            total = jnp.sum(exps, axis=0, keepdims=True)
            item_index = lax.broadcasted_iota(jnp.int32, (chunk, slots), 0)
            matched = item_index == wanted - base
            picked = picked + jnp.sum(jnp.where(matched, scores, 0.0), axis=0, keepdims=True)
            new_max = jnp.maximum(highest, top)
            running = running * jnp.exp(highest - new_max) + total * jnp.exp(top - new_max)
            return (new_max, running, picked)

        return visit

    zero_row = jnp.zeros((1, slots), jnp.float32)
    start_stats = (jnp.full((1, slots), -jnp.inf, jnp.float32), zero_row, zero_row)

    def log_add(a, b):
        top = jnp.maximum(a, b)
        return top + jnp.log(jnp.exp(a - top) + jnp.exp(b - top))

    def stat_mate(part):
        return remote(
            own_stats.at[part],
            mate_stats.at[part],
            stat_mate_send.at[part],
            stat_mate_recv.at[part],
            mate,
        )

    def stat_copy(part, source, peer):
        block = all_stats.at[part, source]
        return remote(
            block, block, stat_send.at[part, peer], stat_recv.at[part, source], chip_device(peer)
        )

    def share_stats(part, found):
        highest, running, picked = found
        own_stats[part, 0:1, :] = highest + jnp.log(running)
        own_stats[part, 1:2, :] = picked
        stat_mate(part).start()

    def spread_stats(part):
        stat_mate(part).wait()
        all_stats[part, chip] = jnp.concatenate(
            [
                log_add(own_stats[part, 0:1, :], mate_stats[part, 0:1, :]),
                own_stats[part, 1:2, :] + mate_stats[part, 1:2, :],
            ],
            axis=0,
        )
        each_peer(lambda peer: stat_copy(part, chip, peer).start())

    def collect_stats(part):
        each_peer(lambda source: stat_copy(part, source, source).wait_recv())
        row_max = all_stats[part, 0, 0:1, :]
        for index in range(1, chips):
            row_max = jnp.maximum(row_max, all_stats[part, index, 0:1, :])
        exp_total = zero_row
        target_score = zero_row
        for index in range(chips):
            exp_total = exp_total + jnp.exp(all_stats[part, index, 0:1, :] - row_max)
            target_score = target_score + all_stats[part, index, 1:2, :]
        log_total = row_max + jnp.log(exp_total)

        @pl.when(core == part)
        def write_losses():
            losses = jnp.broadcast_to(log_total - target_score, (rows, slots))
            row_index = lax.broadcasted_iota(jnp.int32, (rows, slots), 0)
            row_place = lax.broadcasted_iota(jnp.int32, (rows, slots), 1)
            own_losses = jnp.sum(
                jnp.where(row_place == row_index + chip * rows, losses, 0.0),
                axis=1,
                keepdims=True,
            )
            cell_row = lax.broadcasted_iota(jnp.int32, (rows, lanes), 0)
            cell_lane = lax.broadcasted_iota(jnp.int32, (rows, lanes), 1)
            loss_row = jnp.sum(
                jnp.where(
                    cell_row == cell_lane, jnp.broadcast_to(own_losses, (rows, lanes)), 0.0
                ),
                axis=0,
                keepdims=True,
            )
            loss_ref[...] = loss_row[:, :rows]

        return log_total

    def backward_states(part, log_total):
        wanted = part_of(local_target, part)
        part_weight = part_of(weight, part)
        grad_t[...] = jnp.zeros_like(grad_t)

        def visit(index, carried):
            base = pl.multiple_of(index * chunk, chunk)
            factor = part_weight * jnp.exp(chunk_max[part, index] - log_total)
            item_index = lax.broadcasted_iota(jnp.int32, (chunk, slots), 0)
            matched = item_index == wanted - base
            value = probs[part, pl.ds(base, chunk), :] * factor - jnp.where(
                matched, jnp.broadcast_to(part_weight, (chunk, slots)), 0.0
            )
            value = value.astype(jnp.bfloat16)
            signal[part, pl.ds(base, chunk), :] = value
            grad_t[...] += jnp.dot(
                items_t[:, pl.ds(base, chunk)], value, preferred_element_type=jnp.float32
            )
            return carried

        return visit

    grad_mate = remote(grads, mate_grads, grad_mate_sems.at[0], grad_mate_sems.at[1], mate)

    def hand_over(part):
        turned = grad_t[...].T.reshape(chips, rows, width)

        @pl.when(core == part)
        def keep():
            send_grads[...] = turned

        @pl.when(core != part)
        def give():
            grads[...] = turned
            grad_mate.start()

    def grad_copy(source, peer):
        return remote(
            wire_grads.at[peer],
            recv_grads.at[source],
            grad_send.at[peer],
            grad_recv.at[source],
            chip_device(peer),
        )

    def send_out(part):
        @pl.when(core == part)
        def combine():
            grad_mate.wait_recv()
            wire_grads[...] = (send_grads[...] + mate_grads[...]).astype(wire_grads.dtype)
            each_peer(lambda peer: grad_copy(chip, peer).start())
            recv_grads[chip] = wire_grads[chip]

    def out_copy(index):
        span = pl.ds(pl.multiple_of(index * chunk, chunk), chunk)
        return pltpu.make_async_copy(stage.at[span], tgrad_ref.at[span], out_sems.at[index])

    def backward_items(index, carried):
        base = pl.multiple_of(index * chunk, chunk)
        value = jnp.dot(
            signal[0, pl.ds(base, chunk), :], states[0], preferred_element_type=jnp.float32
        ) + jnp.dot(
            signal[1, pl.ds(base, chunk), :], states[1], preferred_element_type=jnp.float32
        )
        stage[pl.ds(base, chunk), :] = value.astype(jnp.bfloat16)
        out_copy(index).start()
        return carried

    early = chunk_count // 2
    share_stats(0, lax.fori_loop(0, chunk_count, forward(0), start_stats))
    found = lax.fori_loop(0, early, forward(1), start_stats)
    spread_stats(0)
    share_stats(1, lax.fori_loop(early, chunk_count, forward(1), found))
    spread_stats(1)
    first_total = collect_stats(0)
    lax.fori_loop(0, chunk_count, backward_states(0, first_total), 0)
    hand_over(0)
    second_total = collect_stats(1)
    visit = backward_states(1, second_total)
    lax.fori_loop(0, early, visit, 0)
    send_out(0)
    lax.fori_loop(early, chunk_count, visit, 0)
    hand_over(1)
    lax.fori_loop(0, early, backward_items, 0)
    send_out(1)
    lax.fori_loop(early, chunk_count, backward_items, 0)

    each_peer(lambda source: grad_copy(source, source).wait_recv())
    total = recv_grads[0].astype(jnp.float32)
    for index in range(1, chips):
        total = total + recv_grads[index].astype(jnp.float32)
    hgrad_ref[...] = total.astype(jnp.bfloat16)

    for copy in sent:
        copy.wait_send()
    for source in all_chips:
        relay_copy(source).wait_send()
    grad_mate.wait_send()

    def finish(peer):
        stat_copy(0, chip, peer).wait_send()
        stat_copy(1, chip, peer).wait_send()
        grad_copy(chip, peer).wait_send()

    each_peer(finish)

    def drain(index, carried):
        out_copy(index).wait()
        return carried

    lax.fori_loop(0, chunk_count, drain, 0)


def fused(item_size, group_size, chunk, wire, hidden, item_table, targets, lengths):
    rows, width = hidden.shape
    half = item_table.shape[0] // group_size
    chips = item_size * group_size // 2
    slots = rows * chips
    chunk_count = half // chunk
    padded = rows + 8
    near_size = 2 if item_size % 4 == 0 else 1
    far_size = item_size // 2 // near_size
    gather_sends = far_size - 1 + far_size * (near_size * group_size - 1)
    vmem = pl.BlockSpec(memory_space=pltpu.VMEM)
    dma = pltpu.SemaphoreType.DMA
    f32, bf16 = jnp.float32, jnp.bfloat16
    loss, hgrad, tgrad = pl.pallas_call(
        functools.partial(fused_kernel, item_size, group_size, near_size, chunk),
        out_shape=(
            jax.ShapeDtypeStruct((1, rows), f32),
            jax.ShapeDtypeStruct((rows, width), bf16),
            jax.ShapeDtypeStruct((half, width), bf16),
        ),
        in_specs=[
            vmem,
            vmem,
            pl.BlockSpec(memory_space=pltpu.SMEM),
            pl.BlockSpec(memory_space=pl.ANY),
        ],
        out_specs=(vmem, vmem, pl.BlockSpec(memory_space=pl.ANY)),
        scratch_shapes=[
            pltpu.VMEM((8, width), jnp.int32),
            pltpu.VMEM((2, chips, padded, width), bf16),
            pltpu.VMEM((2, slots, width), bf16),
            pltpu.VMEM((half, width), bf16),
            pltpu.VMEM((width, half), bf16),
            pltpu.VMEM((2, half, slots), f32),
            pltpu.VMEM((2, half, slots), bf16),
            pltpu.VMEM((2, chunk_count, 1, slots), f32),
            pltpu.VMEM((2, 2, slots), f32),
            pltpu.VMEM((2, 2, slots), f32),
            pltpu.VMEM((2, chips, 2, slots), f32),
            pltpu.VMEM((width, slots), f32),
            pltpu.VMEM((chips, rows, width), f32),
            pltpu.VMEM((chips, rows, width), f32),
            pltpu.VMEM((chips, rows, width), f32),
            pltpu.VMEM((chips, rows, width), wire),
            pltpu.VMEM((chips, rows, width), wire),
            pltpu.VMEM((half, width), bf16),
            dma,
            dma((chunk_count,)),
            dma((gather_sends,)),
            dma((chips,)),
            dma((chips,)),
            dma((chips,)),
            dma((2,)),
            dma((2,)),
            dma((2, chips)),
            dma((2, chips)),
            dma((2,)),
            dma((chips,)),
            dma((chips,)),
        ],
        compiler_params=pltpu.CompilerParams(
            collective_id=0, has_side_effects=True, vmem_limit_bytes=60 * 1024 * 1024
        ),
        name="fused_loss",
    )(hidden, targets.reshape(1, rows), lengths, item_table)
    return loss.reshape(rows), hgrad, tgrad


def solution(mesh):
    in_specs = (P(("grp", "item"), None), P("item", None), P(("grp", "item")), P())
    out_specs = (P(("grp", "item")), P(("grp", "item"), None), P(("item", "grp"), None))
    item_size, group_size = mesh.shape["item"], mesh.shape["grp"]

    def body(hidden, item_table, targets, lengths):
        rows, width = hidden.shape
        half = item_table.shape[0] // group_size
        chunk = min(512, half)
        fits = (
            rows % 8 == 0
            and rows <= 128
            and width % 128 == 0
            and item_size % 2 == 0
            and half * group_size == item_table.shape[0]
            and half % chunk == 0
            and chunk % 128 == 0
            and (rows * item_size * group_size) % 256 == 0
            and (item_size & (item_size - 1)) == 0
            and item_size * item_table.shape[0] <= 1 << 24
        )
        if fits:
            return fused(
                item_size, group_size, chunk, jnp.bfloat16, hidden, item_table, targets, lengths
            )
        return local(hidden, item_table, targets, lengths)

    return jax.shard_map(body, mesh=mesh, in_specs=in_specs, out_specs=out_specs, check_vma=False)
```

```python
import functools
import jax
import jax.numpy as jnp
from jax import lax
from jax.experimental import pallas as pl
from jax.experimental.pallas import tpu as pltpu
from jax.sharding import PartitionSpec as P


def block_width():
    return 2048


def weights_for(lengths, group_index, group_rows):
    seq_count = lengths.shape[1]
    own_lengths = lax.dynamic_index_in_dim(lengths, group_index, 0, keepdims=False)
    seq_ends = jnp.cumsum(own_lengths)
    starts = seq_ends - own_lengths
    places = jnp.arange(group_rows, dtype=jnp.int32)
    inside = (places[:, None] >= starts[None, :]) & (places[:, None] < seq_ends[None, :])
    row_length = jnp.sum(
        jnp.where(inside, own_lengths[None, :].astype(jnp.float32), jnp.float32(0.0)), axis=1
    )
    return group_rows / seq_count / row_length


def split_blocks(item_table, first_item, block_size):
    block_count = item_table.shape[0] // block_size
    blocks = item_table.reshape(block_count, block_size, item_table.shape[1])
    block_starts = first_item + block_size * jnp.arange(block_count, dtype=jnp.int32)
    return (blocks, block_starts)


def partial_stats(states, target_ids, item_table, first_item, block_size):
    blocks, block_starts = split_blocks(item_table, first_item, block_size)
    row_count = states.shape[0]

    def partial_visit(carried, block_pair):
        highest, running, picked = carried
        item_block, block_start = block_pair
        scores = jnp.einsum("rd,id->ri", states, item_block, preferred_element_type=jnp.float32)
        new_max = jnp.maximum(highest, jnp.max(scores, axis=1))
        running = running * jnp.exp(highest - new_max) + jnp.sum(
            jnp.exp(scores - new_max[:, None]), axis=1
        )
        columns = block_start + jnp.arange(block_size, dtype=jnp.int32)
        matched = target_ids[:, None] == columns[None, :]
        picked = picked + jnp.sum(jnp.where(matched, scores, jnp.float32(0.0)), axis=1)
        return ((new_max, running, picked), None)

    start_stats = (
        jnp.full((row_count,), -jnp.inf, dtype=jnp.float32),
        jnp.zeros((row_count,), jnp.float32),
        jnp.zeros((row_count,), jnp.float32),
    )
    final_stats, unused = lax.scan(partial_visit, start_stats, (blocks, block_starts))
    return final_stats


def backward(states, target_ids, item_table, first_item, block_size, log_total, row_weight):
    blocks, block_starts = split_blocks(item_table, first_item, block_size)

    def backward_visit(state_grad, block_pair):
        item_block, block_start = block_pair
        scores = jnp.einsum("rd,id->ri", states, item_block, preferred_element_type=jnp.float32)
        columns = block_start + jnp.arange(block_size, dtype=jnp.int32)
        matched = (target_ids[:, None] == columns[None, :]).astype(jnp.float32)
        signal = (row_weight[:, None] * (jnp.exp(scores - log_total[:, None]) - matched)).astype(
            jnp.bfloat16
        )
        state_grad = state_grad + jnp.dot(signal, item_block, preferred_element_type=jnp.float32)
        item_grad = jnp.einsum("ri,rd->id", signal, states, preferred_element_type=jnp.float32)
        return (state_grad, item_grad)

    start_grad = jnp.zeros((states.shape[0], states.shape[1]), jnp.float32)
    state_grad, item_grads = lax.scan(backward_visit, start_grad, (blocks, block_starts))
    return (state_grad, item_grads.reshape(item_table.shape[0], item_table.shape[1]))


def local(hidden, item_table, targets, lengths):
    rows_local = hidden.shape[0]
    items_local = item_table.shape[0]
    block_size = block_width()
    item_rank = lax.axis_index("item")
    group_rank = lax.axis_index("grp")
    first_item = item_rank * items_local
    group_states, group_targets = (
        lax.all_gather(hidden, "item", axis=0, tiled=True),
        lax.all_gather(targets, "item", axis=0, tiled=True),
    )
    group_rows = group_states.shape[0]
    states, target_ids = (
        lax.all_gather(group_states, "grp", axis=0, tiled=True),
        lax.all_gather(group_targets, "grp", axis=0, tiled=True),
    )
    row_weight = jnp.concatenate(
        [weights_for(lengths, member, group_rows) for member in range(lengths.shape[0])]
    )
    own_start = group_rank * group_rows + item_rank * rows_local
    highest, running, picked = partial_stats(states, target_ids, item_table, first_item, block_size)
    row_max = lax.pmax(highest, "item")
    exp_total, target_score = lax.psum((running * jnp.exp(highest - row_max), picked), "item")
    log_total = row_max + jnp.log(exp_total)
    losses = log_total - target_score
    row_loss = lax.dynamic_slice_in_dim(losses, own_start, rows_local)
    half_items = items_local // 2
    own_items = lax.dynamic_slice_in_dim(item_table, group_rank * half_items, half_items)
    state_grad, table_grad = backward(
        states,
        target_ids,
        own_items,
        first_item + group_rank * half_items,
        block_width(),
        log_total,
        row_weight,
    )
    group_grad = lax.psum_scatter(state_grad, "grp", scatter_dimension=0, tiled=True)
    hidden_grad = lax.psum_scatter(group_grad, "item", scatter_dimension=0, tiled=True)
    return (row_loss, hidden_grad.astype(jnp.bfloat16), table_grad.astype(jnp.bfloat16))


def fused_kernel(
    item_size,
    group_size,
    near_size,
    chunk,
    hidden_ref,
    targets_ref,
    lengths_ref,
    table_ref,
    loss_ref,
    hgrad_ref,
    tgrad_ref,
    target_pad,
    gathered,
    states,
    items,
    probs,
    signal,
    chunk_max,
    own_stats,
    mate_stats,
    all_stats,
    grad_rows,
    grads,
    mate_grads,
    send_grads,
    wire_grads,
    recv_grads,
    stage,
    items_sem,
    out_sems,
    gather_send,
    gather_recv,
    relay_send,
    relay_recv,
    stat_mate_send,
    stat_mate_recv,
    stat_send,
    stat_recv,
    grad_mate_sems,
    grad_send,
    grad_recv,
):
    rows, width = hidden_ref.shape
    half = items.shape[0]
    chunk_count = half // chunk
    padded = gathered.shape[2]
    positions = states.shape[0]
    slots = positions // 2
    chips_per_group = item_size // 2
    chips = chips_per_group * group_size
    far_size = chips_per_group // near_size
    group_rows = rows * item_size
    lanes = 128

    item_rank = lax.axis_index("item")
    group_rank = lax.axis_index("grp")
    core = lax.rem(item_rank, 2)
    in_group = item_rank // 2
    chip = group_rank * chips_per_group + in_group
    near = lax.rem(in_group, near_size)
    far = in_group // near_size
    first_item = (item_rank * group_size + group_rank) * half

    def chip_device(which):
        return {
            "item": 2 * lax.rem(which, chips_per_group) + core,
            "grp": which // chips_per_group,
        }

    mate = {"item": 2 * in_group + 1 - core, "grp": group_rank}

    def remote(src, dst, send_sem, recv_sem, device):
        return pltpu.make_async_remote_copy(
            src_ref=src,
            dst_ref=dst,
            send_sem=send_sem,
            recv_sem=recv_sem,
            device_id=device,
            device_id_type=pl.DeviceIdType.MESH,
        )

    def each_peer(body):
        def step(offset, carried):
            body(lax.rem(chip + offset, chips))
            return carried

        lax.fori_loop(1, chips, step, 0)

    def flipped(offset):
        place = far
        for bit in range(offset.bit_length()):
            size = 1 << bit
            if offset & size:
                place = place + size - 2 * size * lax.rem(far // size, 2)
        return place

    far_places = [flipped(offset) for offset in range(far_size)]
    columns = [
        (lax.rem(near + step_near, near_size), lax.rem(group_rank + step_group, group_size))
        for step_near in range(near_size)
        for step_group in range(group_size)
    ]

    def chip_at(column, place):
        return column[1] * chips_per_group + place * near_size + column[0]

    far_chips = [chip_at(columns[0], place) for place in far_places[1:]]
    near_chips = [chip_at(column, far) for column in columns[1:]]

    items_copy = pltpu.make_async_copy(
        table_ref.at[pl.ds(pl.multiple_of(group_rank * half, chunk), half)], items, items_sem
    )
    items_copy.start()

    barrier = pltpu.get_barrier_semaphore()
    greeted = [mate] + [chip_device(peer) for peer in far_chips + near_chips]
    for device in greeted:
        pl.semaphore_signal(
            barrier, inc=1, device_id=device, device_id_type=pl.DeviceIdType.MESH
        )

    target_pad[...] = jnp.zeros_like(target_pad)
    target_pad[0:1, 0:rows] = targets_ref[...]
    wide_targets = jnp.broadcast_to(target_pad[0:1, :], (8, width))
    digit_row = lax.broadcasted_iota(jnp.int32, (8, width), 0)
    digits = jnp.where(
        digit_row == 0,
        wide_targets & 255,
        jnp.where(
            digit_row == 1,
            (wide_targets >> 8) & 255,
            jnp.where(digit_row == 2, (wide_targets >> 16) & 255, 0),
        ),
    ).astype(jnp.float32)
    gathered[core, chip] = jnp.concatenate(
        [hidden_ref[...].astype(jnp.float32), digits], axis=0
    ).astype(jnp.bfloat16)

    pl.semaphore_wait(barrier, len(greeted))

    def gather_copy(source, lane, peer):
        block = gathered.at[core, source]
        return remote(
            block, block, gather_send.at[lane], gather_recv.at[source], chip_device(peer)
        )

    def relay_copy(source):
        block = gathered.at[core, source]
        return remote(block, block, relay_send.at[source], relay_recv.at[source], mate)

    def relay_arrival(source):
        block = gathered.at[1 - core, source]
        return remote(block, block, relay_send.at[source], relay_recv.at[source], mate)

    sent = []

    def send_on(source, peers):
        for peer in peers:
            copy = gather_copy(source, len(sent), peer)
            copy.start()
            sent.append(copy)

    send_on(chip, far_chips)
    send_on(chip, near_chips)
    relay_copy(chip).start()

    slot_index = lax.broadcasted_iota(jnp.int32, (1, positions), 1)
    slot_block = slot_index // rows
    slot_row = slot_index - slot_block * rows
    slot_chip = lax.rem(slot_block, chips)
    places = (
        (slot_chip // chips_per_group) * item_size
        + 2 * lax.rem(slot_chip, chips_per_group)
        + slot_block // chips
    ) * rows + slot_row
    row_length = jnp.zeros((1, positions), jnp.float32)
    for member in range(group_size):
        start = member * group_rows
        for seq in range(lengths_ref.shape[1]):
            length = lengths_ref[member, seq]
            inside = (places >= start) & (places < start + length)
            row_length = jnp.where(inside, length.astype(jnp.float32), row_length)
            start = start + length
    weight = (group_rows / lengths_ref.shape[1]) / row_length

    lane_index = lax.broadcasted_iota(jnp.int32, (lanes, positions), 0)
    spread = (slot_row == lane_index).astype(jnp.float32).astype(jnp.bfloat16)

    items_copy.wait()

    for source in far_chips:
        gather_copy(source, 0, source).wait_recv()
        send_on(source, near_chips)
        relay_copy(source).start()
    others = [chip_at(column, place) for place in far_places for column in columns[1:]]
    for source in others:
        gather_copy(source, 0, source).wait_recv()
        relay_copy(source).start()
    all_chips = [chip] + far_chips + others
    for source in all_chips:
        relay_arrival(source).wait_recv()

    everything = gathered[...].reshape(2 * chips, padded, width).astype(jnp.float32)
    states[...] = everything[:, :rows, :].reshape(positions, width).astype(jnp.bfloat16)
    code = everything[:, rows:padded, :lanes]
    code_rows = code.shape[0] * code.shape[1]
    code = code.reshape(code_rows, lanes).astype(jnp.bfloat16)
    coded = jnp.dot(code, spread, preferred_element_type=jnp.float32)
    code_index = lax.broadcasted_iota(jnp.int32, (code_rows, positions), 0)
    by_digit = jnp.sum(
        jnp.where(code_index >> 3 == slot_block, coded, 0.0).reshape(2 * chips, 8, positions),
        axis=0,
    )
    target_ids = (
        by_digit[0:1, :] + 256.0 * by_digit[1:2, :] + 65536.0 * by_digit[2:3, :]
    ).astype(jnp.int32)
    local_target = target_ids - first_item

    def part_of(row, part):
        return row[:, part * slots : (part + 1) * slots]

    def forward(part):
        wanted = part_of(local_target, part)

        def visit(index, carried):
            highest, running, picked = carried
            base = pl.multiple_of(index * chunk, chunk)
            scores = lax.dot_general(
                items[pl.ds(base, chunk), :],
                states[part * slots : (part + 1) * slots, :],
                (((1,), (1,)), ((), ())),
                preferred_element_type=jnp.float32,
            )
            top = jnp.max(scores, axis=0, keepdims=True)
            exps = jnp.exp(scores - top)
            probs[part, pl.ds(base, chunk), :] = exps
            chunk_max[part, index] = top
            total = jnp.sum(exps, axis=0, keepdims=True)
            item_index = lax.broadcasted_iota(jnp.int32, (chunk, slots), 0)
            matched = item_index == wanted - base
            picked = picked + jnp.sum(jnp.where(matched, scores, 0.0), axis=0, keepdims=True)
            new_max = jnp.maximum(highest, top)
            running = running * jnp.exp(highest - new_max) + total * jnp.exp(top - new_max)
            return (new_max, running, picked)

        return visit

    zero_row = jnp.zeros((1, slots), jnp.float32)
    start_stats = (jnp.full((1, slots), -jnp.inf, jnp.float32), zero_row, zero_row)

    def log_add(a, b):
        top = jnp.maximum(a, b)
        return top + jnp.log(jnp.exp(a - top) + jnp.exp(b - top))

    def stat_mate(part):
        return remote(
            own_stats.at[part],
            mate_stats.at[part],
            stat_mate_send.at[part],
            stat_mate_recv.at[part],
            mate,
        )

    def stat_copy(part, source, peer):
        block = all_stats.at[part, source]
        return remote(
            block, block, stat_send.at[part, peer], stat_recv.at[part, source], chip_device(peer)
        )

    def share_stats(part, found):
        highest, running, picked = found
        own_stats[part, 0:1, :] = highest + jnp.log(running)
        own_stats[part, 1:2, :] = picked
        stat_mate(part).start()

    def spread_stats(part):
        stat_mate(part).wait()
        all_stats[part, chip] = jnp.concatenate(
            [
                log_add(own_stats[part, 0:1, :], mate_stats[part, 0:1, :]),
                own_stats[part, 1:2, :] + mate_stats[part, 1:2, :],
            ],
            axis=0,
        )
        each_peer(lambda peer: stat_copy(part, chip, peer).start())

    def collect_stats(part):
        each_peer(lambda source: stat_copy(part, source, source).wait_recv())
        row_max = all_stats[part, 0, 0:1, :]
        for index in range(1, chips):
            row_max = jnp.maximum(row_max, all_stats[part, index, 0:1, :])
        exp_total = zero_row
        target_score = zero_row
        for index in range(chips):
            exp_total = exp_total + jnp.exp(all_stats[part, index, 0:1, :] - row_max)
            target_score = target_score + all_stats[part, index, 1:2, :]
        log_total = row_max + jnp.log(exp_total)

        @pl.when(core == part)
        def write_losses():
            losses = jnp.broadcast_to(log_total - target_score, (rows, slots))
            row_index = lax.broadcasted_iota(jnp.int32, (rows, slots), 0)
            row_place = lax.broadcasted_iota(jnp.int32, (rows, slots), 1)
            own_losses = jnp.sum(
                jnp.where(row_place == row_index + chip * rows, losses, 0.0),
                axis=1,
                keepdims=True,
            )
            cell_row = lax.broadcasted_iota(jnp.int32, (rows, lanes), 0)
            cell_lane = lax.broadcasted_iota(jnp.int32, (rows, lanes), 1)
            loss_row = jnp.sum(
                jnp.where(
                    cell_row == cell_lane, jnp.broadcast_to(own_losses, (rows, lanes)), 0.0
                ),
                axis=0,
                keepdims=True,
            )
            loss_ref[...] = loss_row[:, :rows]

        return log_total

    def backward_states(part, log_total):
        wanted = part_of(local_target, part)
        part_weight = part_of(weight, part)
        grad_rows[...] = jnp.zeros_like(grad_rows)

        def visit(index, carried):
            base = pl.multiple_of(index * chunk, chunk)
            factor = part_weight * jnp.exp(chunk_max[part, index] - log_total)
            item_index = lax.broadcasted_iota(jnp.int32, (chunk, slots), 0)
            matched = item_index == wanted - base
            value = probs[part, pl.ds(base, chunk), :] * factor - jnp.where(
                matched, jnp.broadcast_to(part_weight, (chunk, slots)), 0.0
            )
            value = value.astype(jnp.bfloat16)
            signal[pl.ds(base, chunk), part * slots : (part + 1) * slots] = value
            grad_rows[...] += lax.dot_general(
                value,
                items[pl.ds(base, chunk), :],
                (((0,), (0,)), ((), ())),
                preferred_element_type=jnp.float32,
            )
            return carried

        return visit

    grad_mate = remote(grads, mate_grads, grad_mate_sems.at[0], grad_mate_sems.at[1], mate)

    def hand_over(part):
        turned = grad_rows[...].reshape(chips, rows, width)

        @pl.when(core == part)
        def keep():
            send_grads[...] = turned

        @pl.when(core != part)
        def give():
            grads[...] = turned
            grad_mate.start()

    def grad_copy(source, peer):
        return remote(
            wire_grads.at[peer],
            recv_grads.at[source],
            grad_send.at[peer],
            grad_recv.at[source],
            chip_device(peer),
        )

    def send_out(part):
        @pl.when(core == part)
        def combine():
            grad_mate.wait_recv()
            wire_grads[...] = (send_grads[...] + mate_grads[...]).astype(wire_grads.dtype)
            each_peer(lambda peer: grad_copy(chip, peer).start())
            recv_grads[chip] = wire_grads[chip]

    def out_copy(index):
        span = pl.ds(pl.multiple_of(index * chunk, chunk), chunk)
        return pltpu.make_async_copy(stage.at[span], tgrad_ref.at[span], out_sems.at[index])

    def backward_items(index, carried):
        base = pl.multiple_of(index * chunk, chunk)
        value = jnp.dot(
            signal[pl.ds(base, chunk), :], states[...], preferred_element_type=jnp.float32
        )
        stage[pl.ds(base, chunk), :] = value.astype(jnp.bfloat16)
        out_copy(index).start()
        return carried

    early = chunk_count // 2
    share_stats(0, lax.fori_loop(0, chunk_count, forward(0), start_stats, unroll=4))
    found = lax.fori_loop(0, early, forward(1), start_stats, unroll=4)
    spread_stats(0)
    share_stats(1, lax.fori_loop(early, chunk_count, forward(1), found, unroll=4))
    spread_stats(1)
    first_total = collect_stats(0)
    lax.fori_loop(0, chunk_count, backward_states(0, first_total), 0, unroll=4)
    hand_over(0)
    second_total = collect_stats(1)
    visit = backward_states(1, second_total)
    lax.fori_loop(0, early, visit, 0, unroll=4)
    send_out(0)
    lax.fori_loop(early, chunk_count, visit, 0, unroll=4)
    hand_over(1)
    lax.fori_loop(0, early, backward_items, 0, unroll=4)
    send_out(1)
    lax.fori_loop(early, chunk_count, backward_items, 0, unroll=4)

    each_peer(lambda source: grad_copy(source, source).wait_recv())
    total = recv_grads[0].astype(jnp.float32)
    for index in range(1, chips):
        total = total + recv_grads[index].astype(jnp.float32)
    hgrad_ref[...] = total.astype(jnp.bfloat16)

    for copy in sent:
        copy.wait_send()
    for source in all_chips:
        relay_copy(source).wait_send()
    grad_mate.wait_send()

    def finish(peer):
        stat_copy(0, chip, peer).wait_send()
        stat_copy(1, chip, peer).wait_send()
        grad_copy(chip, peer).wait_send()

    each_peer(finish)

    def drain(index, carried):
        out_copy(index).wait()
        return carried

    lax.fori_loop(0, chunk_count, drain, 0)


def hand_out_kernel(loss_in, hgrad_in, tgrad_in, loss_out, hgrad_out, tgrad_out, held, sems, outs):
    count = held.shape[0]
    block = held.shape[1]

    def span(index):
        return pl.ds(index * block, block)

    loads = [
        pltpu.make_async_copy(tgrad_in.at[span(index)], held.at[index], sems.at[index])
        for index in range(count)
    ]
    stores = [
        pltpu.make_async_copy(held.at[index], tgrad_out.at[span(index)], outs.at[index])
        for index in range(count)
    ]
    for load in loads:
        load.start()
    loss_out[...] = loss_in[...]
    hgrad_out[...] = hgrad_in[...]
    for load, store in zip(loads, stores):
        load.wait()
        store.start()
    for store in stores:
        store.wait()


def hand_out(chunk, loss, hgrad, tgrad):
    vmem = pl.BlockSpec(memory_space=pltpu.VMEM)
    whole = pl.BlockSpec(memory_space=pl.ANY)
    count = tgrad.shape[0] // chunk
    return pl.pallas_call(
        hand_out_kernel,
        out_shape=tuple(jax.ShapeDtypeStruct(x.shape, x.dtype) for x in (loss, hgrad, tgrad)),
        in_specs=[vmem, vmem, whole],
        out_specs=(vmem, vmem, whole),
        scratch_shapes=[
            pltpu.VMEM((count, chunk, tgrad.shape[1]), tgrad.dtype),
            pltpu.SemaphoreType.DMA((count,)),
            pltpu.SemaphoreType.DMA((count,)),
        ],
        name="hand_out",
    )(loss, hgrad, tgrad)


def fused(item_size, group_size, chunk, wire, hidden, item_table, targets, lengths):
    rows, width = hidden.shape
    half = item_table.shape[0] // group_size
    chips = item_size * group_size // 2
    slots = rows * chips
    chunk_count = half // chunk
    padded = rows + 8
    near_size = 2 if item_size % 4 == 0 else 1
    far_size = item_size // 2 // near_size
    gather_sends = far_size - 1 + far_size * (near_size * group_size - 1)
    vmem = pl.BlockSpec(memory_space=pltpu.VMEM)
    dma = pltpu.SemaphoreType.DMA
    f32, bf16 = jnp.float32, jnp.bfloat16
    results = pl.pallas_call(
        functools.partial(fused_kernel, item_size, group_size, near_size, chunk),
        out_shape=(
            jax.ShapeDtypeStruct((1, rows), f32),
            jax.ShapeDtypeStruct((rows, width), bf16),
            jax.ShapeDtypeStruct((half, width), bf16),
        ),
        in_specs=[
            vmem,
            vmem,
            pl.BlockSpec(memory_space=pltpu.SMEM),
            pl.BlockSpec(memory_space=pl.ANY),
        ],
        out_specs=(vmem, vmem, pl.BlockSpec(memory_space=pl.ANY)),
        scratch_shapes=[
            pltpu.VMEM((8, width), jnp.int32),
            pltpu.VMEM((2, chips, padded, width), bf16),
            pltpu.VMEM((2 * slots, width), bf16),
            pltpu.VMEM((half, width), bf16),
            pltpu.VMEM((2, half, slots), f32),
            pltpu.VMEM((half, 2 * slots), bf16),
            pltpu.VMEM((2, chunk_count, 1, slots), f32),
            pltpu.VMEM((2, 2, slots), f32),
            pltpu.VMEM((2, 2, slots), f32),
            pltpu.VMEM((2, chips, 2, slots), f32),
            pltpu.VMEM((slots, width), f32),
            pltpu.VMEM((chips, rows, width), f32),
            pltpu.VMEM((chips, rows, width), f32),
            pltpu.VMEM((chips, rows, width), f32),
            pltpu.VMEM((chips, rows, width), wire),
            pltpu.VMEM((chips, rows, width), wire),
            pltpu.VMEM((half, width), bf16),
            dma,
            dma((chunk_count,)),
            dma((gather_sends,)),
            dma((chips,)),
            dma((chips,)),
            dma((chips,)),
            dma((2,)),
            dma((2,)),
            dma((2, chips)),
            dma((2, chips)),
            dma((2,)),
            dma((chips,)),
            dma((chips,)),
        ],
        compiler_params=pltpu.CompilerParams(
            collective_id=0, has_side_effects=True, vmem_limit_bytes=60 * 1024 * 1024
        ),
        name="fused_loss",
    )(hidden, targets.reshape(1, rows), lengths, item_table)
    loss, hgrad, tgrad = hand_out(chunk, *results)
    return loss.reshape(rows), hgrad, tgrad


def solution(mesh):
    in_specs = (P(("grp", "item"), None), P("item", None), P(("grp", "item")), P())
    out_specs = (P(("grp", "item")), P(("grp", "item"), None), P(("item", "grp"), None))
    item_size, group_size = mesh.shape["item"], mesh.shape["grp"]

    def body(hidden, item_table, targets, lengths):
        rows, width = hidden.shape
        half = item_table.shape[0] // group_size
        chunk = min(512, half)
        fits = (
            rows % 8 == 0
            and rows <= 128
            and width % 128 == 0
            and item_size % 2 == 0
            and half * group_size == item_table.shape[0]
            and half % chunk == 0
            and chunk % 128 == 0
            and (rows * item_size * group_size) % 256 == 0
            and (item_size & (item_size - 1)) == 0
            and item_size * item_table.shape[0] <= 1 << 24
        )
        if fits:
            return fused(
                item_size, group_size, chunk, jnp.bfloat16, hidden, item_table, targets, lengths
            )
        return local(hidden, item_table, targets, lengths)

    return jax.shard_map(body, mesh=mesh, in_specs=in_specs, out_specs=out_specs, check_vma=False)
```
